32 devices in a mesh: shard: 8 (over z, x), tensor: 4 (over y, core).
Axes of the slice: x: 2, y: 2, z: 4, core: 2. Of those that a mesh axis runs over, the one named last changes fastest.
Arguments:
- matrix_grads: bfloat16 [56, 512, 2560], P(None, 'shard', 'tensor'), may hold values from -64 to 64
- matrix_momentum: float32 [56, 512, 2560], P(None, 'shard', 'tensor'), may hold values from -64 to 64
- matrix_weights: float32 [56, 512, 2560], P(None, 'shard', 'tensor'), may hold values from -6 to 6
- table_grads: bfloat16 [2048, 2560], P('shard', 'tensor'), may hold values from -6 to 6
- table_state: float32 [3, 2048, 2560], P(None, 'shard', 'tensor'), may hold values from -4 to 4, as said below
- small_grads: bfloat16 [120, 2560], P(None, 'tensor'), may hold values from -6 to 6
- small_state: float32 [3, 120, 2560], P(None, None, 'tensor'), may hold values from -4 to 4, as said below
Outputs:
- matrix_update: float32 [56, 512, 2560], P(None, 'shard', 'tensor')
- momentum_next: float32 [56, 512, 2560], P(None, 'shard', 'tensor')
- table_out: float32 [2, 2048, 2560], P(None, 'shard', 'tensor')
- small_out: float32 [2, 120, 2560], P(None, None, 'tensor')
The draws below stay inside these ranges and needn't reach their ends.
Inputs may be any that keep to these rules, and one draw needn't show every extreme that they name: `table_state`: index 0 holds weights, index 1 first moments, index 2 second moments, which lie between 0.0002 and 0.004. `small_state`: index 0 holds weights, index 1 first moments, index 2 second moments, which lie between 0.0002 and 0.004.
All inputs are finite; a program needn't handle non-finite values.
Results may differ from the reference program's by a relative error of at most 0.014.
The reference program's roundings to bfloat16 on the way count: a program that leaves them out, or rounds other values in their place, can miss the bound.
Values may be sent and summed in bfloat16 or wider, within the bound.
A program may use at most 192 MiB of HBM per device.

```python
import math
import jax
import jax.numpy as jnp
from jax import lax

D = 2560
KV = 512
EXPERTS = 64
ITERS = 5
NMAT = 56
EMB = 2048
SMALL = 120


def matrix_scales(key):
    base_key = jax.random.fold_in(key, 11)
    row_key, col_key = jax.random.split(base_key)
    rising = 3.0 ** (jnp.arange(KV, dtype=jnp.float32) / (KV - 1))
    row_rough = jnp.exp(jax.random.uniform(row_key, (NMAT, KV), jnp.float32, 0.0, math.log(3.5)))
    col_rough = jnp.exp(jax.random.uniform(col_key, (NMAT, 1, D), jnp.float32, 0.0, math.log(10.0)))
    return (rising[None, :] * row_rough)[:, :, None] * col_rough


def matrix_entries(key, salt):
    scales = matrix_scales(key)
    noise_key = jax.random.fold_in(key, salt)
    noise = jax.random.truncated_normal(noise_key, -4.0, 4.0, (NMAT, KV, D), jnp.float32)
    return 0.1 * noise * scales


def draw_matrix_grads(key, part):
    return matrix_entries(key, 1).astype(jnp.bfloat16)


def draw_matrix_momentum(key, part):
    return matrix_entries(key, 2)


def adam_entries(key, rows):
    weight_key, moment_key, second_key = jax.random.split(key, 3)
    weights = jax.random.truncated_normal(weight_key, -4.0, 4.0, (rows, D), jnp.float32)
    moments = 0.3 * jax.random.truncated_normal(moment_key, -4.0, 4.0, (rows, D), jnp.float32)
    seconds = jnp.exp(jax.random.uniform(second_key, (rows, D), jnp.float32, math.log(0.0002), math.log(0.004)))
    return jnp.stack([weights, moments, seconds])


def draw_table_state(key, part):
    return adam_entries(jax.random.fold_in(key, 21), EMB)


def draw_small_state(key, part):
    return adam_entries(jax.random.fold_in(key, 22), SMALL)


def shard_levels(key, dims, cuts, smallest, high):
    def one(axis_at, shards_of):
        heights = jax.random.uniform(jax.random.fold_in(jax.random.fold_in(key, 6), axis_at), (shards_of,), jnp.float32, smallest / len(cuts), high / len(cuts))
        return jnp.repeat(jnp.exp(heights), dims[axis_at] // shards_of).reshape((-1,) + (1,) * (len(dims) - axis_at - 1))

    loudness = one(*cuts[0])
    for cut in cuts[1:]:
        loudness = loudness * one(*cut)
    return loudness


def normal_values(key, extent, width, most, cuts=(), held_as=jnp.bfloat16):
    entries = width * jax.random.normal(key, extent, jnp.float32)
    if cuts:
        entries = entries * shard_levels(key, extent, cuts, -0.22, 0.18)
    return jnp.clip(entries, -most, most).astype(held_as)


def setup_inputs(seed: int = 0) -> dict:
    seeds = jax.random.split(jax.random.key(seed), 8)
    matrix_grads = draw_matrix_grads(jax.random.fold_in(seeds[7], 71), 0)
    matrix_momentum = draw_matrix_momentum(jax.random.fold_in(seeds[7], 71), 0)
    matrix_weights = normal_values(seeds[2], (NMAT, KV, D), 1.0, 6.0, ((1, 8), (2, 4)), jnp.float32)
    table_grads = normal_values(seeds[3], (EMB, D), 1.0, 6.0, ((0, 8), (1, 4)))
    table_state = draw_table_state(jax.random.fold_in(seeds[7], 71), 0)
    small_grads = normal_values(seeds[5], (SMALL, D), 1.0, 6.0, ((1, 4),))
    small_state = draw_small_state(jax.random.fold_in(seeds[7], 71), 0)
    return {"matrix_grads": matrix_grads, "matrix_momentum": matrix_momentum, "matrix_weights": matrix_weights, "table_grads": table_grads, "table_state": table_state, "small_grads": small_grads, "small_state": small_state}


COEF_A = 3.4445
COEF_B = -4.775
COEF_C = 2.0315
BIAS_ONE = 1.0 - 0.9 ** 10
BIAS_TWO = 1.0 - 0.999 ** 10

def newton_schulz(blended):
    squares = jnp.sum(jnp.square(blended.astype(jnp.float32)))
    iterate = (blended.astype(jnp.float32) / (jnp.sqrt(squares) + 1e-07)).astype(jnp.bfloat16)
    iterate = lax.optimization_barrier(iterate)
    for turn in range(ITERS):
        gram_matrix = jnp.dot(iterate, iterate.T, preferred_element_type=jnp.float32).astype(jnp.bfloat16)
        gram_matrix = lax.optimization_barrier(gram_matrix)
        gram_square = jnp.dot(gram_matrix, gram_matrix, preferred_element_type=jnp.float32)
        polynomial = (COEF_B * gram_matrix.astype(jnp.float32) + COEF_C * gram_square).astype(jnp.bfloat16)
        iterate = (COEF_A * iterate.astype(jnp.float32) + jnp.dot(polynomial, iterate, preferred_element_type=jnp.float32)).astype(jnp.bfloat16)
        iterate = lax.optimization_barrier(iterate)
    return iterate

def adamw(gradient, states, decay_rate):
    grad_value = gradient.astype(jnp.float32)
    moment_one = 0.9 * states[1] + 0.1 * grad_value
    moment_two = 0.999 * states[2] + 0.001 * grad_value * grad_value
    direction = moment_one / BIAS_ONE / (jnp.sqrt(moment_two / BIAS_TWO) + 1e-08) + decay_rate * states[0]
    return jnp.stack([direction, moment_one])

def reference(matrix_grads, matrix_momentum, matrix_weights, table_grads, table_state, small_grads, small_state):
    momentum_next = 0.95 * matrix_momentum + matrix_grads.astype(jnp.float32)
    blended = (matrix_grads.astype(jnp.float32) + 0.95 * momentum_next).astype(jnp.bfloat16)
    blended = lax.optimization_barrier(blended)
    orthogonal = lax.map(newton_schulz, blended)
    muon_scale = 0.2 * math.sqrt(max(KV, D))
    matrix_update = muon_scale * orthogonal.astype(jnp.float32) + 0.1 * matrix_weights
    table_out = adamw(table_grads, table_state, 0.1)
    row_index = jnp.arange(small_grads.shape[0], dtype=jnp.int32)
    small_decay = jnp.where(row_index < EXPERTS, 0.1, 0.0).astype(jnp.float32)[:, None]
    small_out = adamw(small_grads, small_state, small_decay)
    return (matrix_update, momentum_next, table_out, small_out)
```

```python
import functools
import math

import jax
import jax.numpy as jnp
from jax import lax
from jax.experimental import pallas as pl
from jax.experimental.pallas import tpu as pltpu
from jax.sharding import PartitionSpec as P

D = 2560
KV = 512
EXPERTS = 64
ITERS = 5


COEF_A = 3.4445
COEF_B = -4.775
COEF_C = 2.0315
BIAS_ONE = 1.0 - 0.9**10
BIAS_TWO = 1.0 - 0.999**10

CHUNK = 512
MESH = pl.DeviceIdType.MESH


def orthogonalize(x, gram, root, poly):
    rows, cols = x.shape
    chunks = cols // CHUNK

    def columns(c):
        return pl.ds(pl.multiple_of(c * CHUNK, CHUNK), CHUNK)

    def add_squares(c, total):
        part = jnp.square(x[:, columns(c)].astype(jnp.float32))
        return total + jnp.sum(part, keepdims=True)

    squares = lax.fori_loop(0, chunks, add_squares, jnp.zeros((1, 1), jnp.float32))
    norm = jnp.sqrt(squares) + 1e-07

    def add_gram(part):
        gram[...] += lax.dot_general(
            part, part, (((1,), (1,)), ((), ())), preferred_element_type=jnp.float32
        )

    gram[...] = jnp.zeros_like(gram)

    def scale(c, carry):
        part = (x[:, columns(c)].astype(jnp.float32) / norm).astype(jnp.bfloat16)
        x[:, columns(c)] = part
        add_gram(part)
        return carry

    lax.fori_loop(0, chunks, scale, 0)

    def turn(t, carry):
        root[...] = gram[...].astype(jnp.bfloat16)
        square = jnp.dot(root[...], root[...], preferred_element_type=jnp.float32)
        poly[...] = (COEF_B * root[...].astype(jnp.float32) + COEF_C * square).astype(jnp.bfloat16)
        gram[...] = jnp.zeros_like(gram)

        def step(c, inner):
            part = x[:, columns(c)]
            product = jnp.dot(poly[...], part, preferred_element_type=jnp.float32)
            part = (COEF_A * part.astype(jnp.float32) + product).astype(jnp.bfloat16)
            x[:, columns(c)] = part

            @pl.when(t < ITERS - 1)
            def _():
                add_gram(part)

            return inner

        lax.fori_loop(0, chunks, step, 0)
        return carry

    lax.fori_loop(0, ITERS, turn, 0)


def muon_kernel(
    sizes,
    blended,
    result,
    whole,
    gram,
    root,
    poly,
    out_sem,
    in_sem,
    back_out_sem,
    back_in_sem,
):
    shards, tensor_size = sizes
    devices = shards * tensor_size
    count, rows, cols = blended.shape
    slots = whole.shape[0]
    shard = lax.axis_index("shard")
    tensor = lax.axis_index("tensor")
    me = shard * tensor_size + tensor
    last = slots - 1
    remainder = count - last * devices
    mine_last = (me * remainder + devices - 1) // devices
    has_last = (mine_last < remainder) & ((mine_last * devices) // remainder == me)

    def place(device):
        return (device // tensor_size, device % tensor_size)

    def block(slot, device):
        at_row, at_col = place(device)
        return whole.at[
            slot,
            pl.ds(pl.multiple_of(at_row * rows, rows), rows),
            pl.ds(pl.multiple_of(at_col * cols, cols), cols),
        ]

    barrier = pltpu.get_barrier_semaphore()

    def greet(i, carry):
        pl.semaphore_signal(
            barrier, inc=1, device_id=place((me + i) % devices), device_id_type=MESH
        )
        return carry

    lax.fori_loop(1, devices, greet, 0)
    pl.semaphore_wait(barrier, devices - 1)

    def outbound(slot, k, held):
        m = slot * devices + k
        home = (k * devices) // held
        return m, home, pltpu.make_async_remote_copy(
            src_ref=blended.at[m],
            dst_ref=block(slot, me),
            send_sem=out_sem.at[m],
            recv_sem=in_sem.at[slot],
            device_id=place(home),
            device_id_type=MESH,
        )

    for slot in range(slots):
        held = devices if slot < last else remainder
        first = (me * held) // devices

        def send(i, carry, slot=slot, held=held, first=first):
            k = (first + i) % held
            m, home, copy = outbound(slot, k, held)

            @pl.when(home != me)
            def _():
                copy.start()

            @pl.when(home == me)
            def _():
                pltpu.make_async_copy(blended.at[m], block(slot, me), in_sem.at[slot]).start()

            return carry

        lax.fori_loop(0, held, send, 0)

    def backward(slot, m, target):
        return pltpu.make_async_remote_copy(
            src_ref=block(slot, target),
            dst_ref=result.at[m],
            send_sem=back_out_sem.at[slot, target],
            recv_sem=back_in_sem.at[m],
            device_id=place(target),
            device_id_type=MESH,
        )

    def work(slot, carry):
        @pl.when((slot < last) | has_last)
        def _():
            m = slot * devices + jnp.where(slot < last, me, mine_last)
            whole_slot = whole.at[slot]
            pltpu.make_async_copy(whole_slot, whole_slot, in_sem.at[slot]).wait()
            orthogonalize(whole_slot, gram, root, poly)

            def send_back(i, inner):
                target = (me + i) % devices
                backward(slot, m, target).start()
                return inner

            lax.fori_loop(1, devices, send_back, 0)
            pltpu.make_async_copy(block(slot, me), result.at[m], back_in_sem.at[m]).start()

        return carry

    lax.fori_loop(0, slots, work, 0)

    for slot in range(slots):
        held = devices if slot < last else remainder

        def sent(k, carry, slot=slot, held=held):
            m, home, copy = outbound(slot, k, held)

            @pl.when(home != me)
            def _():
                copy.wait_send()

            return carry

        lax.fori_loop(0, held, sent, 0)

    def sent_back(slot, carry):
        @pl.when((slot < last) | has_last)
        def _():
            m = slot * devices + jnp.where(slot < last, me, mine_last)

            def one(i, inner):
                backward(slot, m, (me + i) % devices).wait_send()
                return inner

            lax.fori_loop(1, devices, one, 0)

        return carry

    lax.fori_loop(0, slots, sent_back, 0)

    def returned(m, carry):
        pltpu.make_async_copy(result.at[m], result.at[m], back_in_sem.at[m]).wait()
        return carry

    lax.fori_loop(0, count, returned, 0)


def muon(blended):
    shards = lax.axis_size("shard")
    tensor_size = lax.axis_size("tensor")
    devices = shards * tensor_size
    count, rows, cols = blended.shape
    slots = -(-count // devices)
    full_rows, full_cols = rows * shards, cols * tensor_size
    return pl.pallas_call(
        functools.partial(muon_kernel, (shards, tensor_size)),
        out_shape=jax.ShapeDtypeStruct(blended.shape, jnp.bfloat16),
        in_specs=[pl.BlockSpec(memory_space=pl.ANY)],
        out_specs=pl.BlockSpec(memory_space=pl.ANY),
        scratch_shapes=[
            pltpu.VMEM((slots, full_rows, full_cols), jnp.bfloat16),
            pltpu.VMEM((full_rows, full_rows), jnp.float32),
            pltpu.VMEM((full_rows, full_rows), jnp.bfloat16),
            pltpu.VMEM((full_rows, full_rows), jnp.bfloat16),
            pltpu.SemaphoreType.DMA((count,)),
            pltpu.SemaphoreType.DMA((slots,)),
            pltpu.SemaphoreType.DMA((slots, devices)),
            pltpu.SemaphoreType.DMA((count,)),
        ],
        compiler_params=pltpu.CompilerParams(
            collective_id=0, has_side_effects=True, vmem_limit_bytes=40 * 1024 * 1024
        ),
        name="muon",
    )(blended)


def adamw(gradient, states, decay_rate):
    grad_value = gradient.astype(jnp.float32)
    moment_one = 0.9 * states[1] + 0.1 * grad_value
    moment_two = 0.999 * states[2] + 0.001 * grad_value * grad_value
    direction = (
        moment_one / BIAS_ONE / (jnp.sqrt(moment_two / BIAS_TWO) + 1e-08) + decay_rate * states[0]
    )
    return jnp.stack([direction, moment_one])


def local(
    matrix_grads,
    matrix_momentum,
    matrix_weights,
    table_grads,
    table_state,
    small_grads,
    small_state,
):
    momentum_next = 0.95 * matrix_momentum + matrix_grads.astype(jnp.float32)
    blended = (matrix_grads.astype(jnp.float32) + 0.95 * momentum_next).astype(jnp.bfloat16)
    orthogonal = muon(blended)
    muon_scale = 0.2 * math.sqrt(max(KV, D))
    matrix_update = muon_scale * orthogonal.astype(jnp.float32) + 0.1 * matrix_weights
    table_out = adamw(table_grads, table_state, 0.1)
    row_index = jnp.arange(small_grads.shape[0], dtype=jnp.int32)
    small_decay = jnp.where(row_index < EXPERTS, 0.1, 0.0).astype(jnp.float32)[:, None]
    small_out = adamw(small_grads, small_state, small_decay)
    return (matrix_update, momentum_next, table_out, small_out)


def solution(mesh):
    placed = (
        P(None, "shard", "tensor"),
        P(None, "shard", "tensor"),
        P(None, "shard", "tensor"),
        P("shard", "tensor"),
        P(None, "shard", "tensor"),
        P(None, "tensor"),
        P(None, None, "tensor"),
    )
    return jax.shard_map(
        local,
        mesh=mesh,
        in_specs=placed,
        out_specs=(
            P(None, "shard", "tensor"),
            P(None, "shard", "tensor"),
            P(None, "shard", "tensor"),
            P(None, None, "tensor"),
        ),
        check_vma=False,
    )
```

```python
import functools
import math

import jax
import jax.numpy as jnp
from jax import lax
from jax.experimental import pallas as pl
from jax.experimental.pallas import tpu as pltpu
from jax.sharding import PartitionSpec as P

D = 2560
KV = 512
EXPERTS = 64
ITERS = 5


COEF_A = 3.4445
COEF_B = -4.775
COEF_C = 2.0315
BIAS_ONE = 1.0 - 0.9**10
BIAS_TWO = 1.0 - 0.999**10

CHUNK = 512
MESH = pl.DeviceIdType.MESH


def orthogonalize(x, gram, root, poly):
    rows, cols = x.shape
    chunks = cols // CHUNK

    def columns(c):
        return pl.ds(pl.multiple_of(c * CHUNK, CHUNK), CHUNK)

    def add_squares(c, total):
        part = jnp.square(x[:, columns(c)].astype(jnp.float32))
        return total + jnp.sum(part, keepdims=True)

    squares = lax.fori_loop(0, chunks, add_squares, jnp.zeros((1, 1), jnp.float32))
    norm = jnp.sqrt(squares) + 1e-07

    def add_gram(part):
        gram[...] += lax.dot_general(
            part, part, (((1,), (1,)), ((), ())), preferred_element_type=jnp.float32
        )

    gram[...] = jnp.zeros_like(gram)

    def scale(c, carry):
        part = (x[:, columns(c)].astype(jnp.float32) / norm).astype(jnp.bfloat16)
        x[:, columns(c)] = part
        add_gram(part)
        return carry

    lax.fori_loop(0, chunks, scale, 0)

    def turn(t, carry):
        root[...] = gram[...].astype(jnp.bfloat16)
        square = jnp.dot(root[...], root[...], preferred_element_type=jnp.float32)
        poly[...] = (COEF_B * root[...].astype(jnp.float32) + COEF_C * square).astype(jnp.bfloat16)
        gram[...] = jnp.zeros_like(gram)

        def step(c, inner):
            part = x[:, columns(c)]
            product = jnp.dot(poly[...], part, preferred_element_type=jnp.float32)
            part = (COEF_A * part.astype(jnp.float32) + product).astype(jnp.bfloat16)
            x[:, columns(c)] = part

            @pl.when(t < ITERS - 1)
            def _():
                add_gram(part)

            return inner

        lax.fori_loop(0, chunks, step, 0)
        return carry

    lax.fori_loop(0, ITERS, turn, 0)


LANES = 8
OUT_STRIDE = 5
BACK_STRIDE = 13


def rotation(step, first, held, stride):
    while math.gcd(stride, held) > 1:
        stride += 1
    return (first + (step + 1) * stride) % held


def inverse(step, first, held, stride):
    while math.gcd(stride, held) > 1:
        stride += 1
    return (first + (held - 1 - step) * stride) % held


def muon_kernel(
    sizes,
    grads,
    momentum,
    weights,
    update,
    momentum_next,
    whole,
    gram,
    root,
    poly,
    blended,
    result,
    grad_lane,
    read_lane,
    write_lane,
    grad_sem,
    read_sem,
    write_sem,
    out_sem,
    in_sem,
    back_out_sem,
    back_in_sem,
):
    shards, tensor_size = sizes
    devices = shards * tensor_size
    count, rows, cols = grads.shape
    slots = whole.shape[0]
    shard = lax.axis_index("shard")
    tensor = lax.axis_index("tensor")
    me = shard * tensor_size + tensor
    last = slots - 1
    remainder = count - last * devices
    mine_last = (me * remainder + devices - 1) // devices
    has_last = (mine_last < remainder) & ((mine_last * devices) // remainder == me)
    muon_scale = 0.2 * math.sqrt(max(whole.shape[1], whole.shape[2]))
    lanes = grad_lane.shape[0]

    def place(device):
        return (device // tensor_size, device % tensor_size)

    def block(slot, device):
        at_row, at_col = place(device)
        return whole.at[
            slot,
            pl.ds(pl.multiple_of(at_row * rows, rows), rows),
            pl.ds(pl.multiple_of(at_col * cols, cols), cols),
        ]

    def item(i, back):
        slot = i // devices
        step = i % devices
        first = (me * remainder) // devices
        if back:
            k_full = inverse(step, me, devices, BACK_STRIDE)
            k_last = inverse(step % remainder, first, remainder, BACK_STRIDE)
        else:
            k_full = rotation(step, me, devices, OUT_STRIDE)
            k_last = rotation(step, first, remainder, OUT_STRIDE)
        k = jnp.where(slot < last, k_full, k_last)
        home = jnp.where(slot < last, k_full, (k_last * devices) // remainder)
        return slot, slot * devices + k, home

    def read_grads(i):
        m = item(i, False)[1]
        lane = i % lanes
        return pltpu.make_async_copy(grads.at[m], grad_lane.at[lane], grad_sem.at[lane])

    def read_from(source, i, back):
        m = item(i, back)[1]
        lane = i % lanes
        return pltpu.make_async_copy(source.at[m], read_lane.at[lane], read_sem.at[lane])

    def write_to(target, i, back):
        m = item(i, back)[1]
        lane = i % lanes
        return pltpu.make_async_copy(write_lane.at[lane], target.at[m], write_sem.at[lane])

    def open_blend(i, carry):
        read_grads(i).start()
        read_from(momentum, i, False).start()
        return carry

    lax.fori_loop(0, lanes, open_blend, 0)

    barrier = pltpu.get_barrier_semaphore()

    def greet(i, carry):
        pl.semaphore_signal(
            barrier, inc=1, device_id=place((me + i) % devices), device_id_type=MESH
        )
        return carry

    lax.fori_loop(1, devices, greet, 0)
    pl.semaphore_wait(barrier, devices - 1)

    def outbound(slot, m, home):
        return pltpu.make_async_remote_copy(
            src_ref=blended.at[m],
            dst_ref=block(slot, me),
            send_sem=out_sem.at[m],
            recv_sem=in_sem.at[slot],
            device_id=place(home),
            device_id_type=MESH,
        )

    def blend(i, carry):
        slot, m, home = item(i, False)
        lane = i % lanes
        read_grads(i).wait()
        read_from(momentum, i, False).wait()

        @pl.when(i >= lanes)
        def _():
            write_to(momentum_next, i - lanes, False).wait()

        grad = grad_lane[lane].astype(jnp.float32)
        moment = 0.95 * read_lane[lane] + grad
        write_lane[lane] = moment
        blended[m] = (grad + 0.95 * moment).astype(jnp.bfloat16)
        write_to(momentum_next, i, False).start()

        @pl.when(home != me)
        def _():
            outbound(slot, m, home).start()

        @pl.when(home == me)
        def _():
            pltpu.make_async_copy(blended.at[m], block(slot, me), in_sem.at[slot]).start()

        @pl.when(i + lanes < count)
        def _():
            read_grads(i + lanes).start()
            read_from(momentum, i + lanes, False).start()

        return carry

    lax.fori_loop(0, count, blend, 0)

    def close_blend(i, carry):
        write_to(momentum_next, i, False).wait()
        return carry

    lax.fori_loop(count - lanes, count, close_blend, 0)

    def open_update(i, carry):
        read_from(weights, i, True).start()
        return carry

    lax.fori_loop(0, lanes, open_update, 0)

    def backward(slot, m, target):
        return pltpu.make_async_remote_copy(
            src_ref=block(slot, target),
            dst_ref=result.at[m],
            send_sem=back_out_sem.at[slot, target],
            recv_sem=back_in_sem.at[m],
            device_id=place(target),
            device_id_type=MESH,
        )

    def work(slot, carry):
        @pl.when((slot < last) | has_last)
        def _():
            m = slot * devices + jnp.where(slot < last, me, mine_last)
            whole_slot = whole.at[slot]
            pltpu.make_async_copy(whole_slot, whole_slot, in_sem.at[slot]).wait()
            orthogonalize(whole_slot, gram, root, poly)

            def send_back(i, inner):
                target = rotation(i, me, devices, BACK_STRIDE)

                @pl.when(target != me)
                def _():
                    backward(slot, m, target).start()

                return inner

            lax.fori_loop(0, devices, send_back, 0)
            pltpu.make_async_copy(block(slot, me), result.at[m], back_in_sem.at[m]).start()

        return carry

    lax.fori_loop(0, slots, work, 0)

    def finish(i, carry):
        m = item(i, True)[1]
        lane = i % lanes
        read_from(weights, i, True).wait()
        pltpu.make_async_copy(result.at[m], result.at[m], back_in_sem.at[m]).wait()

        @pl.when(i >= lanes)
        def _():
            write_to(update, i - lanes, True).wait()

        write_lane[lane] = muon_scale * result[m].astype(jnp.float32) + 0.1 * read_lane[lane]
        write_to(update, i, True).start()

        @pl.when(i + lanes < count)
        def _():
            read_from(weights, i + lanes, True).start()

        return carry

    lax.fori_loop(0, count, finish, 0)

    def sent(i, carry):
        slot, m, home = item(i, False)

        @pl.when(home != me)
        def _():
            outbound(slot, m, home).wait_send()

        return carry

    lax.fori_loop(0, count, sent, 0)

    def sent_back(slot, carry):
        @pl.when((slot < last) | has_last)
        def _():
            m = slot * devices + jnp.where(slot < last, me, mine_last)

            def one(i, inner):
                backward(slot, m, (me + i) % devices).wait_send()
                return inner

            lax.fori_loop(1, devices, one, 0)

        return carry

    lax.fori_loop(0, slots, sent_back, 0)

    def close_update(i, carry):
        write_to(update, i, True).wait()
        return carry

    lax.fori_loop(count - lanes, count, close_update, 0)


def muon(grads, momentum, weights):
    shards = lax.axis_size("shard")
    tensor_size = lax.axis_size("tensor")
    devices = shards * tensor_size
    count, rows, cols = grads.shape
    slots = -(-count // devices)
    full_rows, full_cols = rows * shards, cols * tensor_size
    lanes = min(LANES, count)
    anywhere = pl.BlockSpec(memory_space=pl.ANY)
    return pl.pallas_call(
        functools.partial(muon_kernel, (shards, tensor_size)),
        out_shape=[jax.ShapeDtypeStruct(grads.shape, jnp.float32)] * 2,
        in_specs=[pl.BlockSpec(memory_space=pltpu.HBM)] * 3,
        out_specs=[anywhere] * 2,
        scratch_shapes=[
            pltpu.VMEM((slots, full_rows, full_cols), jnp.bfloat16),
            pltpu.VMEM((full_rows, full_rows), jnp.float32),
            pltpu.VMEM((full_rows, full_rows), jnp.bfloat16),
            pltpu.VMEM((full_rows, full_rows), jnp.bfloat16),
            pltpu.VMEM((count, rows, cols), jnp.bfloat16),
            pltpu.VMEM((count, rows, cols), jnp.bfloat16),
            pltpu.VMEM((lanes, rows, cols), jnp.bfloat16),
            pltpu.VMEM((lanes, rows, cols), jnp.float32),
            pltpu.VMEM((lanes, rows, cols), jnp.float32),
            pltpu.SemaphoreType.DMA((lanes,)),
            pltpu.SemaphoreType.DMA((lanes,)),
            pltpu.SemaphoreType.DMA((lanes,)),
            pltpu.SemaphoreType.DMA((count,)),
            pltpu.SemaphoreType.DMA((slots,)),
            pltpu.SemaphoreType.DMA((slots, devices)),
            pltpu.SemaphoreType.DMA((count,)),
        ],
        compiler_params=pltpu.CompilerParams(
            collective_id=0, has_side_effects=True, vmem_limit_bytes=28 * 1024 * 1024
        ),
        name="muon",
    )(grads, momentum, weights)


def adamw(gradient, states, decay_rate):
    grad_value = gradient.astype(jnp.float32)
    moment_one = 0.9 * states[1] + 0.1 * grad_value
    moment_two = 0.999 * states[2] + 0.001 * grad_value * grad_value
    direction = (
        moment_one / BIAS_ONE / (jnp.sqrt(moment_two / BIAS_TWO) + 1e-08) + decay_rate * states[0]
    )
    return jnp.stack([direction, moment_one])


def local(
    matrix_grads,
    matrix_momentum,
    matrix_weights,
    table_grads,
    table_state,
    small_grads,
    small_state,
):
    matrix_update, momentum_next = muon(matrix_grads, matrix_momentum, matrix_weights)
    table_out = adamw(table_grads, table_state, 0.1)
    row_index = jnp.arange(small_grads.shape[0], dtype=jnp.int32)
    small_decay = jnp.where(row_index < EXPERTS, 0.1, 0.0).astype(jnp.float32)[:, None]
    small_out = adamw(small_grads, small_state, small_decay)
    return (matrix_update, momentum_next, table_out, small_out)


def solution(mesh):
    placed = (
        P(None, "shard", "tensor"),
        P(None, "shard", "tensor"),
        P(None, "shard", "tensor"),
        P("shard", "tensor"),
        P(None, "shard", "tensor"),
        P(None, "tensor"),
        P(None, None, "tensor"),
    )
    return jax.shard_map(
        local,
        mesh=mesh,
        in_specs=placed,
        out_specs=(
            P(None, "shard", "tensor"),
            P(None, "shard", "tensor"),
            P(None, "shard", "tensor"),
            P(None, None, "tensor"),
        ),
        check_vma=False,
    )
```

```python
import functools
import math

import jax
import jax.numpy as jnp
from jax import lax
from jax.experimental import pallas as pl
from jax.experimental.pallas import tpu as pltpu
from jax.sharding import PartitionSpec as P

D = 2560
KV = 512
EXPERTS = 64
ITERS = 5


COEF_A = 3.4445
COEF_B = -4.775
COEF_C = 2.0315
BIAS_ONE = 1.0 - 0.9**10
BIAS_TWO = 1.0 - 0.999**10

CHUNK = 512
MESH = pl.DeviceIdType.MESH


def orthogonalize(x, gram, root, poly):
    rows, cols = x.shape
    chunks = cols // CHUNK

    def columns(c):
        return pl.ds(pl.multiple_of(c * CHUNK, CHUNK), CHUNK)

    def add_squares(c, total):
        part = jnp.square(x[:, columns(c)].astype(jnp.float32))
        return total + jnp.sum(part, keepdims=True)

    squares = lax.fori_loop(0, chunks, add_squares, jnp.zeros((1, 1), jnp.float32))
    norm = jnp.sqrt(squares) + 1e-07

    def add_gram(part):
        gram[...] += lax.dot_general(
            part, part, (((1,), (1,)), ((), ())), preferred_element_type=jnp.float32
        )

    gram[...] = jnp.zeros_like(gram)

    def scale(c, carry):
        part = (x[:, columns(c)].astype(jnp.float32) / norm).astype(jnp.bfloat16)
        x[:, columns(c)] = part
        add_gram(part)
        return carry

    lax.fori_loop(0, chunks, scale, 0)

    def turn(t, carry):
        root[...] = gram[...].astype(jnp.bfloat16)
        square = jnp.dot(root[...], root[...], preferred_element_type=jnp.float32)
        poly[...] = (COEF_B * root[...].astype(jnp.float32) + COEF_C * square).astype(jnp.bfloat16)
        gram[...] = jnp.zeros_like(gram)

        def step(c, inner):
            part = x[:, columns(c)]
            product = jnp.dot(poly[...], part, preferred_element_type=jnp.float32)
            part = (COEF_A * part.astype(jnp.float32) + product).astype(jnp.bfloat16)
            x[:, columns(c)] = part

            @pl.when(t < ITERS - 1)
            def _():
                add_gram(part)

            return inner

        lax.fori_loop(0, chunks, step, 0)
        return carry

    lax.fori_loop(0, ITERS, turn, 0)


LANES = 8
OUT_STRIDE = 5
BACK_STRIDE = 13


def rotation(step, first, held, stride):
    while math.gcd(stride, held) > 1:
        stride += 1
    return (first + (step + 1) * stride) % held


def inverse(step, first, held, stride):
    while math.gcd(stride, held) > 1:
        stride += 1
    return (first + (held - 1 - step) * stride) % held


def tilt(shard, tensor_size):
    return (shard // 2) % 2 * (tensor_size // 2)


def muon_kernel(
    sizes,
    grads,
    momentum,
    weights,
    update,
    momentum_next,
    whole,
    gram,
    root,
    poly,
    blended,
    result,
    grad_lane,
    read_lane,
    write_lane,
    grad_sem,
    read_sem,
    write_sem,
    out_sem,
    in_sem,
    back_out_sem,
    back_in_sem,
):
    shards, tensor_size = sizes
    devices = shards * tensor_size
    count, rows, cols = grads.shape
    slots = whole.shape[0]
    shard = lax.axis_index("shard")
    tensor = lax.axis_index("tensor")
    me = shard * tensor_size + tensor
    last = slots - 1
    remainder = count - last * devices
    turned = shard * tensor_size + (tensor + tensor_size - tilt(shard, tensor_size)) % tensor_size
    mine_last = (turned * remainder + devices - 1) // devices
    has_last = (mine_last < remainder) & ((mine_last * devices) // remainder == turned)
    muon_scale = 0.2 * math.sqrt(max(whole.shape[1], whole.shape[2]))
    lanes = grad_lane.shape[0]

    def place(device):
        return (device // tensor_size, device % tensor_size)

    def block(slot, device):
        at_row, at_col = place(device)
        return whole.at[
            slot,
            pl.ds(pl.multiple_of(at_row * rows, rows), rows),
            pl.ds(pl.multiple_of(at_col * cols, cols), cols),
        ]

    def item(i, back):
        slot = i // devices
        step = i % devices
        first = (me * remainder) // devices
        if back:
            k_full = inverse(step, me, devices, BACK_STRIDE)
            k_last = inverse(step % remainder, first, remainder, BACK_STRIDE)
        else:
            k_full = rotation(step, me, devices, OUT_STRIDE)
            k_last = rotation(step, first, remainder, OUT_STRIDE)
        k = jnp.where(slot < last, k_full, k_last)
        at = (k_last * devices) // remainder
        row, col = at // tensor_size, at % tensor_size
        spread = row * tensor_size + (col + tilt(row, tensor_size)) % tensor_size
        home = jnp.where(slot < last, k_full, spread)
        return slot, slot * devices + k, home

    def read_grads(i):
        m = item(i, False)[1]
        lane = i % lanes
        return pltpu.make_async_copy(grads.at[m], grad_lane.at[lane], grad_sem.at[lane])

    def read_from(source, i, back):
        m = item(i, back)[1]
        lane = i % lanes
        return pltpu.make_async_copy(source.at[m], read_lane.at[lane], read_sem.at[lane])

    def write_to(target, i, back):
        m = item(i, back)[1]
        lane = i % lanes
        return pltpu.make_async_copy(write_lane.at[lane], target.at[m], write_sem.at[lane])

    def open_blend(i, carry):
        read_grads(i).start()
        read_from(momentum, i, False).start()
        return carry

    lax.fori_loop(0, lanes, open_blend, 0)

    barrier = pltpu.get_barrier_semaphore()

    def greet(i, carry):
        pl.semaphore_signal(
            barrier, inc=1, device_id=place((me + i) % devices), device_id_type=MESH
        )
        return carry

    lax.fori_loop(1, devices, greet, 0)
    pl.semaphore_wait(barrier, devices - 1)

    def outbound(slot, m, home):
        return pltpu.make_async_remote_copy(
            src_ref=blended.at[m],
            dst_ref=block(slot, me),
            send_sem=out_sem.at[m],
            recv_sem=in_sem.at[slot],
            device_id=place(home),
            device_id_type=MESH,
        )

    def send(i, carry):
        slot, m, home = item(i, False)

        @pl.when(home != me)
        def _():
            outbound(slot, m, home).start()

        @pl.when(home == me)
        def _():
            pltpu.make_async_copy(blended.at[m], block(slot, me), in_sem.at[slot]).start()

        return carry

    def arrival(slot):
        pltpu.make_async_copy(whole.at[slot], whole.at[slot], in_sem.at[slot]).wait()

    def blend(i, carry):
        m = item(i, False)[1]
        lane = i % lanes
        read_grads(i).wait()
        read_from(momentum, i, False).wait()

        @pl.when(i >= lanes)
        def _():
            write_to(momentum_next, i - lanes, False).wait()

        grad = grad_lane[lane].astype(jnp.float32)
        moment = 0.95 * read_lane[lane] + grad
        write_lane[lane] = moment
        blended[m] = (grad + 0.95 * moment).astype(jnp.bfloat16)
        write_to(momentum_next, i, False).start()

        @pl.when(i < devices)
        def _():
            send(i, 0)

        @pl.when(i + lanes < count)
        def _():
            read_grads(i + lanes).start()
            read_from(momentum, i + lanes, False).start()

        return carry

    lax.fori_loop(0, count, blend, 0)

    def close_blend(i, carry):
        write_to(momentum_next, i, False).wait()
        return carry

    lax.fori_loop(count - lanes, count, close_blend, 0)

    def open_update(i, carry):
        read_from(weights, i, True).start()
        return carry

    lax.fori_loop(0, lanes, open_update, 0)

    for slot in range(1, slots):
        arrival(slot - 1)
        lax.fori_loop(slot * devices, min((slot + 1) * devices, count), send, 0)

    def backward(slot, m, target):
        return pltpu.make_async_remote_copy(
            src_ref=block(slot, target),
            dst_ref=result.at[m],
            send_sem=back_out_sem.at[slot, target],
            recv_sem=back_in_sem.at[m],
            device_id=place(target),
            device_id_type=MESH,
        )

    def work(slot, carry):
        @pl.when((slot < last) | has_last)
        def _():
            m = slot * devices + jnp.where(slot < last, me, mine_last)
            whole_slot = whole.at[slot]

            @pl.when(slot == last)
            def _():
                arrival(last)

            orthogonalize(whole_slot, gram, root, poly)

            def send_back(i, inner):
                target = rotation(i, me, devices, BACK_STRIDE)

                @pl.when(target != me)
                def _():
                    backward(slot, m, target).start()

                return inner

            lax.fori_loop(0, devices, send_back, 0)
            pltpu.make_async_copy(block(slot, me), result.at[m], back_in_sem.at[m]).start()

        return carry

    lax.fori_loop(0, slots, work, 0)

    def finish(i, carry):
        m = item(i, True)[1]
        lane = i % lanes
        read_from(weights, i, True).wait()
        pltpu.make_async_copy(result.at[m], result.at[m], back_in_sem.at[m]).wait()

        @pl.when(i >= lanes)
        def _():
            write_to(update, i - lanes, True).wait()

        write_lane[lane] = muon_scale * result[m].astype(jnp.float32) + 0.1 * read_lane[lane]
        write_to(update, i, True).start()

        @pl.when(i + lanes < count)
        def _():
            read_from(weights, i + lanes, True).start()

        return carry

    lax.fori_loop(0, count, finish, 0)

    def sent(i, carry):
        slot, m, home = item(i, False)

        @pl.when(home != me)
        def _():
            outbound(slot, m, home).wait_send()

        return carry

    lax.fori_loop(0, count, sent, 0)

    def sent_back(slot, carry):
        @pl.when((slot < last) | has_last)
        def _():
            m = slot * devices + jnp.where(slot < last, me, mine_last)

            def one(i, inner):
                backward(slot, m, (me + i) % devices).wait_send()
                return inner

            lax.fori_loop(1, devices, one, 0)

        return carry

    lax.fori_loop(0, slots, sent_back, 0)

    def close_update(i, carry):
        write_to(update, i, True).wait()
        return carry

    lax.fori_loop(count - lanes, count, close_update, 0)


def muon(grads, momentum, weights):
    shards = lax.axis_size("shard")
    tensor_size = lax.axis_size("tensor")
    devices = shards * tensor_size
    count, rows, cols = grads.shape
    slots = -(-count // devices)
    full_rows, full_cols = rows * shards, cols * tensor_size
    lanes = min(LANES, count)
    anywhere = pl.BlockSpec(memory_space=pl.ANY)
    return pl.pallas_call(
        functools.partial(muon_kernel, (shards, tensor_size)),
        out_shape=[jax.ShapeDtypeStruct(grads.shape, jnp.float32)] * 2,
        in_specs=[pl.BlockSpec(memory_space=pltpu.HBM)] * 3,
        out_specs=[anywhere] * 2,
        scratch_shapes=[
            pltpu.VMEM((slots, full_rows, full_cols), jnp.bfloat16),
            pltpu.VMEM((full_rows, full_rows), jnp.float32),
            pltpu.VMEM((full_rows, full_rows), jnp.bfloat16),
            pltpu.VMEM((full_rows, full_rows), jnp.bfloat16),
            pltpu.VMEM((count, rows, cols), jnp.bfloat16),
            pltpu.VMEM((count, rows, cols), jnp.bfloat16),
            pltpu.VMEM((lanes, rows, cols), jnp.bfloat16),
            pltpu.VMEM((lanes, rows, cols), jnp.float32),
            pltpu.VMEM((lanes, rows, cols), jnp.float32),
            pltpu.SemaphoreType.DMA((lanes,)),
            pltpu.SemaphoreType.DMA((lanes,)),
            pltpu.SemaphoreType.DMA((lanes,)),
            pltpu.SemaphoreType.DMA((count,)),
            pltpu.SemaphoreType.DMA((slots,)),
            pltpu.SemaphoreType.DMA((slots, devices)),
            pltpu.SemaphoreType.DMA((count,)),
        ],
        compiler_params=pltpu.CompilerParams(
            collective_id=0, has_side_effects=True, vmem_limit_bytes=28 * 1024 * 1024
        ),
        name="muon",
    )(grads, momentum, weights)


def adamw(gradient, states, decay_rate):
    grad_value = gradient.astype(jnp.float32)
    moment_one = 0.9 * states[1] + 0.1 * grad_value
    moment_two = 0.999 * states[2] + 0.001 * grad_value * grad_value
    direction = (
        moment_one / BIAS_ONE / (jnp.sqrt(moment_two / BIAS_TWO) + 1e-08) + decay_rate * states[0]
    )
    return jnp.stack([direction, moment_one])


def local(
    matrix_grads,
    matrix_momentum,
    matrix_weights,
    table_grads,
    table_state,
    small_grads,
    small_state,
):
    matrix_update, momentum_next = muon(matrix_grads, matrix_momentum, matrix_weights)
    table_out = adamw(table_grads, table_state, 0.1)
    row_index = jnp.arange(small_grads.shape[0], dtype=jnp.int32)
    small_decay = jnp.where(row_index < EXPERTS, 0.1, 0.0).astype(jnp.float32)[:, None]
    small_out = adamw(small_grads, small_state, small_decay)
    return (matrix_update, momentum_next, table_out, small_out)


def solution(mesh):
    placed = (
        P(None, "shard", "tensor"),
        P(None, "shard", "tensor"),
        P(None, "shard", "tensor"),
        P("shard", "tensor"),
        P(None, "shard", "tensor"),
        P(None, "tensor"),
        P(None, None, "tensor"),
    )
    return jax.shard_map(
        local,
        mesh=mesh,
        in_specs=placed,
        out_specs=(
            P(None, "shard", "tensor"),
            P(None, "shard", "tensor"),
            P(None, "shard", "tensor"),
            P(None, None, "tensor"),
        ),
        check_vma=False,
    )
```
